256 devices in a mesh: dp: 8 (over x_hi, y), fsdp: 16 (over z, core), tensor: 2 (over x_lo).
Axes of the slice: x: 4 (x_hi: 2, x_lo: 2; x = x_hi * 2 + x_lo), y: 4, z: 8, core: 2. Of those that a mesh axis runs over, the one named last changes fastest.
Arguments:
- attn_out: bfloat16 [16384, 2560], P(('dp', 'fsdp')), may hold values from -6 to 6
- cotangent: bfloat16 [16384, 5120], P(('dp', 'fsdp'), 'tensor'), may hold values from -6 to 6
- old_weights: bfloat16 [3, 2048, 4096], P(None, 'tensor', 'fsdp'), may hold values from -0.125 to 0.125
- depth_coef: float32 [2], replicated, may hold values from 0.3 to 1
- depth_pick: int32 [2], replicated, may hold values from 0 to 2
- in_blocks: bfloat16 [20, 2, 128, 128], replicated, may hold values from -0.3125 to 0.3125
- in_cols: int32 [20, 2], replicated, may hold values from 0 to 15, all different within a row
- out_blocks: bfloat16 [40, 2, 128, 128], P('tensor'), may hold values from -0.375 to 0.375
- out_cols: int32 [40, 2], P('tensor'), may hold values from 0 to 31, all different within a row
Outputs:
- grown_out: bfloat16 [16384, 5120], P(('dp', 'fsdp'), 'tensor')
- grad_attn: bfloat16 [16384, 2560], P(('dp', 'fsdp'), 'tensor')
- grad_in_blocks: float32 [20, 2, 128, 128], P('tensor')
- grad_out_blocks: float32 [40, 2, 128, 128], P('tensor')
The draws below stay inside these ranges and needn't reach their ends.
Inputs may be any that keep to these rules, and one draw needn't show every extreme that they name: `in_cols`: each row names 2 different old head blocks; every old head block is named by some row. `out_cols`: each row names 2 different old width blocks; every old width block is named by some row.
All inputs are finite; a program needn't handle non-finite values.
Results may differ from the reference program's by a relative error of at most 0.0095.
Values may be sent and summed in bfloat16 or wider, within the bound.
No kernel may reach another device: no remote copies, remote signals or barrier semaphores. Data moves between devices by JAX's collectives and lax.ppermute only.
A program may use at most 64 MiB of HBM per device.

```python
import jax
import jax.numpy as jnp
from jax import lax

HEAD = 128
D_OLD = 4096
D_NEW = 5120
HG_OLD = 16
HG_NEW = 20
L_OLD = 3
DEPTH_K = 2
K_IN = 2
K_OUT = 2
TOK_DEV = 128
TOKENS = 16384
F_OLD = 2048
F_NEW = 2560
BO_OLD = 32
BO_NEW = 40
N_TENSOR = 2


def level_of(key, extent, shards, low, largest):
    factor_of, own = 1.0, jax.random.fold_in(key, 6)
    for dim, blocks in shards:
        draws = jnp.exp(jax.random.uniform(jax.random.fold_in(own, dim), (blocks,), jnp.float32, low / len(shards), largest / len(shards)))
        factor_of = factor_of * jnp.repeat(draws, extent[dim] // blocks).reshape([-1 if axis == dim else 1 for axis in range(len(extent))])
    return factor_of


def different_ones(stream_key, rows, count, top, lift):
    ranking = jax.random.permutation(jax.random.fold_in(stream_key, 1), count)
    pull = ranking
    for power in range(3):
        pull = pull * pull // count
    pull = pull * lift // count
    lots = jax.random.randint(jax.random.fold_in(stream_key, 2), (rows, count), 0, 4096) + pull
    fixed_rows = jax.random.permutation(jax.random.fold_in(stream_key, 3), rows)[jnp.arange(count) % rows]
    lots = jnp.where(jnp.arange(rows)[:, None] == fixed_rows[None, :], 1 << 14, lots)
    priority = lots * count + jnp.arange(count)
    return lax.top_k(priority.astype(jnp.int32), top)[1].astype(jnp.int32)


def bell_draw(key, dims, width, reach, shards=(), kind=jnp.bfloat16):
    values = jax.random.normal(key, dims, jnp.float32) * width
    if len(shards) > 0:
        values = level_of(key, dims, shards, -0.22, 0.18) * values
    return jnp.clip(values, min=-reach, max=reach).astype(kind)


def setup_inputs(seed: int = 0) -> dict:
    streams_of = jax.random.split(jax.random.key(seed), 10)
    return {
        "attn_out": bell_draw(streams_of[0], (TOKENS, F_NEW), 1.0, 6.0, ((0, 128),)),
        "cotangent": bell_draw(streams_of[1], (TOKENS, D_NEW), 1.0, 6.0, ((0, 128), (1, 2))),
        "old_weights": bell_draw(streams_of[2], (L_OLD, F_OLD, D_OLD), F_OLD ** -0.5, 0.125, ((1, 2), (2, 16))),
        "depth_coef": jnp.clip(jax.random.uniform(streams_of[3], (DEPTH_K,), jnp.float32, 0.3, 1.0), 0.3, 1.0),
        "depth_pick": jax.random.randint(streams_of[4], (DEPTH_K,), 0, L_OLD).astype(jnp.int32),
        "in_blocks": bell_draw(streams_of[5], (HG_NEW, K_IN, HEAD, HEAD), (HEAD * K_IN * HG_NEW // HG_OLD) ** -0.5, 0.3125),
        "in_cols": different_ones(streams_of[6], HG_NEW, HG_OLD, K_IN, 0),
        "out_blocks": bell_draw(streams_of[7], (BO_NEW, K_OUT, HEAD, HEAD), (HEAD * K_OUT) ** -0.5, 0.375, ((0, 2),)),
        "out_cols": different_ones(streams_of[8], BO_NEW, BO_OLD, K_OUT, 0),
    }


def reference(attn_out, cotangent, old_weights, depth_coef, depth_pick, in_blocks, in_cols, out_blocks, out_cols):
    highest = lax.Precision.HIGHEST
    mixed_weight = jnp.zeros((F_OLD, D_OLD), jnp.float32)
    for layer_slot in range(DEPTH_K):
        picked = lax.dynamic_index_in_dim(old_weights, depth_pick[layer_slot], 0, keepdims=False)
        mixed_weight = mixed_weight + depth_coef[layer_slot] * picked.astype(jnp.float32)
    mixed_weight = mixed_weight.astype(jnp.bfloat16)
    mix_halves = mixed_weight.astype(jnp.float32).reshape(N_TENSOR, F_OLD // N_TENSOR, D_OLD)
    in_hot = (in_cols[:, :, None] == jnp.arange(HG_OLD, dtype=jnp.int32)[None, None, :]).astype(jnp.float32)
    out_hot = (out_cols[:, :, None] == jnp.arange(BO_OLD, dtype=jnp.int32)[None, None, :]).astype(jnp.float32)
    out_hot_halves = out_hot.reshape(N_TENSOR, BO_NEW // N_TENSOR, K_OUT, BO_OLD)
    in_weights = in_blocks.astype(jnp.float32)
    out_weights = out_blocks.astype(jnp.float32)
    out_halves = out_weights.reshape(N_TENSOR, BO_NEW // N_TENSOR, K_OUT, HEAD, HEAD)

    def token_block(totals, pieces):
        attn_rows, cot_rows = pieces
        attn_three = attn_rows.reshape(-1, HG_NEW, HEAD).astype(jnp.float32)
        products = jnp.einsum('trd,rkde->trke', attn_three, in_weights, precision=highest)
        hidden = jnp.einsum('trke,rkc->tce', products, in_hot, precision=highest).reshape(-1, F_OLD).astype(jnp.bfloat16)
        hidden_halves = hidden.astype(jnp.float32).reshape(-1, N_TENSOR, F_OLD // N_TENSOR)
        partials = jnp.einsum('tsf,sfo->tso', hidden_halves, mix_halves, precision=highest).astype(jnp.bfloat16)
        partials = lax.optimization_barrier(partials)
        old_out = jnp.sum(partials.astype(jnp.float32), axis=1).astype(jnp.bfloat16)
        old_selected = jnp.take(old_out.reshape(-1, BO_OLD, HEAD), out_cols, axis=1).astype(jnp.float32)
        grown = jnp.einsum('trkd,rkde->tre', old_selected, out_weights, precision=highest).reshape(-1, D_NEW).astype(jnp.bfloat16)
        cot_four = cot_rows.reshape(-1, N_TENSOR, BO_NEW // N_TENSOR, HEAD).astype(jnp.float32)
        backward_terms = jnp.einsum('tsre,srkde->tsrkd', cot_four, out_halves, precision=highest)
        grad_parts = jnp.einsum('tsrkd,srkc->tscd', backward_terms, out_hot_halves, precision=highest)
        grad_parts = grad_parts.reshape(-1, N_TENSOR, D_OLD).astype(jnp.bfloat16)
        grad_parts = lax.optimization_barrier(grad_parts)
        old_grad = jnp.sum(grad_parts.astype(jnp.float32), axis=1).astype(jnp.bfloat16)
        hidden_grad = jnp.dot(old_grad, mixed_weight.T, preferred_element_type=jnp.float32).astype(jnp.bfloat16)
        grad_selected = jnp.take(hidden_grad.reshape(-1, HG_OLD, HEAD), in_cols, axis=1).astype(jnp.float32)
        grad_attn = jnp.einsum('trke,rkde->trd', grad_selected, in_weights, precision=highest).reshape(-1, F_NEW).astype(jnp.bfloat16)
        in_terms = jnp.einsum('trd,trke->rkde', attn_three, grad_selected, precision=highest)
        cot_three = cot_rows.reshape(-1, BO_NEW, HEAD).astype(jnp.float32)
        out_terms = jnp.einsum('trkd,tre->rkde', old_selected, cot_three, precision=highest)
        return (totals[0] + in_terms, totals[1] + out_terms), (grown, grad_attn)

    attn_split = attn_out.reshape(TOKENS // TOK_DEV, TOK_DEV, F_NEW)
    cot_split = cotangent.reshape(TOKENS // TOK_DEV, TOK_DEV, D_NEW)
    start = (jnp.zeros((HG_NEW, K_IN, HEAD, HEAD), jnp.float32), jnp.zeros((BO_NEW, K_OUT, HEAD, HEAD), jnp.float32))
    sums, outputs = lax.scan(token_block, start, (attn_split, cot_split))
    grad_scale = jnp.float32(TOKENS) ** -0.5
    grown_out = outputs[0].reshape(TOKENS, D_NEW)
    grad_attn = outputs[1].reshape(TOKENS, F_NEW)
    return grown_out, grad_attn, sums[0] * grad_scale, sums[1] * grad_scale
```

```python
import jax
import jax.numpy as jnp
from jax import lax
from jax.sharding import Mesh
from jax.sharding import PartitionSpec as P

HEAD = 128
D_OLD = 4096
HG_OLD = 16
HG_NEW = 20
DEPTH_K = 2
BO_OLD = 32


PEERS = ("xh", "y", "z")


def gathered_mix(mixed_weight):
    return lax.all_gather(mixed_weight, ("z", "c"), axis=1, tiled=True)


def pair_sum(part):
    other = lax.ppermute(part, "xl", [(0, 1), (1, 0)])
    return (part.astype(jnp.float32) + other.astype(jnp.float32)).astype(jnp.bfloat16)


def token_sum(in_terms, out_terms, scale):
    core = lax.axis_index("c")
    peers = lax.axis_size(PEERS)
    ri, ro = in_terms.shape[0] // 2, out_terms.shape[0] // 2

    def half(which):
        a = lax.dynamic_slice_in_dim(in_terms, which * ri, ri, 0).reshape(-1, HEAD)
        b = lax.dynamic_slice_in_dim(out_terms, which * ro, ro, 0).reshape(-1, HEAD)
        return jnp.concatenate([a, b], axis=0)

    swap = [(0, 1), (1, 0)]
    other = lax.ppermute(half(1 - core).astype(jnp.bfloat16), "c", swap)
    mine = (half(core) + other.astype(jnp.float32)).astype(jnp.bfloat16)
    rows = mine.shape[0]
    mine = mine.reshape(peers, rows // peers, HEAD)
    parts = lax.all_to_all(mine, PEERS, 0, 0, tiled=True)
    total = (jnp.sum(parts.astype(jnp.float32), axis=0) * scale).astype(jnp.bfloat16)
    spread = jnp.broadcast_to(total[None], mine.shape)
    full = lax.all_to_all(spread, PEERS, 0, 0, tiled=True).reshape(rows, HEAD)
    theirs = lax.ppermute(full, "c", swap)
    first = jnp.where(core == 0, full, theirs).astype(jnp.float32)
    second = jnp.where(core == 0, theirs, full).astype(jnp.float32)
    cut = ri * in_terms.shape[1] * HEAD
    in_sum = jnp.concatenate([first[:cut], second[:cut]], 0).reshape(in_terms.shape)
    out_sum = jnp.concatenate([first[cut:], second[cut:]], 0).reshape(out_terms.shape)
    return in_sum, out_sum


def local(
    attn_out,
    cotangent,
    old_weights,
    depth_coef,
    depth_pick,
    in_blocks,
    in_cols,
    out_blocks,
    out_cols,
):
    highest = lax.Precision.HIGHEST
    tok_rows = attn_out.shape[0]
    tensor_half = lax.axis_index("xl")
    tensor_count = lax.axis_size("xl")
    local_old = old_weights.shape[1]
    local_blocks = local_old // HEAD
    rows_in = HG_NEW // tensor_count
    mixed_weight = jnp.zeros(old_weights.shape[1:], jnp.float32)
    for layer_slot in range(DEPTH_K):
        picked = lax.dynamic_index_in_dim(old_weights, depth_pick[layer_slot], 0, keepdims=False)
        mixed_weight = mixed_weight + depth_coef[layer_slot] * picked.astype(jnp.float32)
    mixed_weight = mixed_weight.astype(jnp.bfloat16)
    attn_blocks = attn_out.reshape(tok_rows, HG_NEW, HEAD)
    products = jnp.einsum(
        "trd,rkde->trke", attn_blocks, in_blocks, preferred_element_type=jnp.float32
    )
    local_cols = tensor_half * local_blocks + jnp.arange(local_blocks, dtype=jnp.int32)
    in_hot = (in_cols[:, :, None] == local_cols[None, None, :]).astype(jnp.float32)
    hidden_local = jnp.einsum("trke,rkc->tce", products, in_hot, precision=highest)
    hidden_local = hidden_local.reshape(tok_rows, local_old).astype(jnp.bfloat16)
    full_mix = gathered_mix(mixed_weight)
    old_part = jnp.dot(hidden_local, full_mix, preferred_element_type=jnp.float32)
    old_out = pair_sum(old_part.astype(jnp.bfloat16))
    old_selected = jnp.take(old_out.reshape(tok_rows, BO_OLD, HEAD), out_cols, axis=1)
    grown_out = jnp.einsum(
        "trkd,rkde->tre", old_selected, out_blocks, preferred_element_type=jnp.float32
    )
    grown_out = grown_out.reshape(tok_rows, -1).astype(jnp.bfloat16)
    cot_blocks = cotangent.reshape(tok_rows, out_blocks.shape[0], HEAD)
    backward_terms = jnp.einsum(
        "tre,rkde->trkd", cot_blocks, out_blocks, preferred_element_type=jnp.float32
    )
    out_hot = (out_cols[:, :, None] == jnp.arange(BO_OLD, dtype=jnp.int32)[None, None, :]).astype(
        jnp.float32
    )
    grad_part = jnp.einsum("trkd,rkc->tcd", backward_terms, out_hot, precision=highest).reshape(
        tok_rows, D_OLD
    )
    old_grad = pair_sum(grad_part.astype(jnp.bfloat16))
    hidden_grad_local = jnp.einsum(
        "to,fo->tf", old_grad, full_mix, preferred_element_type=jnp.float32
    ).astype(jnp.bfloat16)
    hidden_grad = lax.all_gather(hidden_grad_local, "xl", axis=1, tiled=True)
    my_in_blocks = lax.dynamic_slice_in_dim(in_blocks, tensor_half * rows_in, rows_in, 0)
    my_in_cols = lax.dynamic_slice_in_dim(in_cols, tensor_half * rows_in, rows_in, 0)
    grad_selected = jnp.take(hidden_grad.reshape(tok_rows, HG_OLD, HEAD), my_in_cols, axis=1)
    grad_attn = jnp.einsum(
        "trke,rkde->trd", grad_selected, my_in_blocks, preferred_element_type=jnp.float32
    )
    grad_attn = grad_attn.reshape(tok_rows, rows_in * HEAD).astype(jnp.bfloat16)
    my_attn = lax.dynamic_slice_in_dim(attn_blocks, tensor_half * rows_in, rows_in, 1)
    in_terms = jnp.einsum(
        "trd,trke->rkde", my_attn, grad_selected, preferred_element_type=jnp.float32
    )
    out_terms = jnp.einsum(
        "trkd,tre->rkde", old_selected, cot_blocks, preferred_element_type=jnp.float32
    )
    grad_scale = float(tok_rows * lax.axis_size(PEERS) * lax.axis_size("c")) ** (-0.5)
    in_sum, out_sum = token_sum(in_terms, out_terms, grad_scale)
    return (grown_out, grad_attn, in_sum, out_sum)


def solution(mesh):
    fine = Mesh(mesh.devices.reshape(2, 4, 8, 2, 2), ("xh", "y", "z", "c", "xl"))
    tokens = ("xh", "y", "z", "c")
    placed = (
        P(tokens, None),
        P(tokens, "xl"),
        P(None, "xl", ("z", "c")),
        P(),
        P(),
        P(),
        P(),
        P("xl", None, None, None),
        P("xl", None),
    )
    return jax.shard_map(
        local,
        mesh=fine,
        in_specs=placed,
        out_specs=(
            P(tokens, "xl"),
            P(tokens, "xl"),
            P("xl", None, None, None),
            P("xl", None, None, None),
        ),
        check_vma=False,
    )
```

```python
import jax
import jax.numpy as jnp
from jax import lax
from jax.experimental import pallas as pl
from jax.experimental.pallas import tpu as pltpu
from jax.sharding import Mesh
from jax.sharding import PartitionSpec as P

HEAD = 128
D_OLD = 4096
HG_OLD = 16
HG_NEW = 20
L_OLD = 3
DEPTH_K = 2
BO_OLD = 32
PAIR = [(0, 1), (1, 0)]


def swap_cores(x):
    return lax.ppermute(x, "c", PAIR)


def swap_halves(x):
    return lax.ppermute(x, "xl", PAIR)


def add_pair(mine, other):
    return (mine.astype(jnp.float32) + other.astype(jnp.float32)).astype(jnp.bfloat16)


def arrival_place(cols):
    shard = cols // 2
    away = (shard // 2 - lax.axis_index("z")) % lax.axis_size("z")
    base = jnp.where(away < 4, 8 * away, 60 - 8 * away)
    return base + 2 * (shard % 2 != lax.axis_index("c")) + cols % 2


def forward(x, piece):
    if isinstance(piece, tuple):
        half = piece[0].shape[0]
        return forward(x[:, :half], piece[0]) + forward(x[:, half:], piece[1])
    return jnp.dot(x, piece, preferred_element_type=jnp.float32)


def backward(g, piece):
    if isinstance(piece, tuple):
        return jnp.concatenate([backward(g, part) for part in piece], axis=1)
    return lax.dot_general(
        g, piece, (((1,), (1,)), ((), ())), preferred_element_type=jnp.float32
    )


SMEM = pl.BlockSpec(memory_space=pltpu.SMEM)


def times(x, w, dims):
    return lax.dot_general(x, w, (dims, ((), ())), preferred_element_type=jnp.float32)


def scatter_blocks(x, blocks, place, slots, used, transposed):
    rows = blocks.shape[0]
    tok = x.shape[0]

    def kernel(place_ref, x_ref, w_ref, o_ref, acc_ref):
        acc_ref[...] = jnp.zeros_like(acc_ref)
        for r in range(rows):
            xr = x_ref[:, r * HEAD : (r + 1) * HEAD]
            if transposed:
                both = times(xr, w_ref[r].reshape(2 * HEAD, HEAD), ((1,), (1,)))
            else:
                both = times(xr, jnp.concatenate([w_ref[r, 0], w_ref[r, 1]], 1), ((1,), (0,)))
            for k in range(2):
                c = place_ref[r, k]
                acc_ref[c] = acc_ref[c] + both[:, k * HEAD : (k + 1) * HEAD]
        for c in range(used):
            o_ref[:, c * HEAD : (c + 1) * HEAD] = acc_ref[c].astype(jnp.bfloat16)

    full = pl.BlockSpec(memory_space=pltpu.VMEM)
    return pl.pallas_call(
        kernel,
        out_shape=jax.ShapeDtypeStruct((tok, used * HEAD), jnp.bfloat16),
        in_specs=[SMEM, full, full],
        out_specs=full,
        scratch_shapes=[pltpu.VMEM((slots, tok, HEAD), jnp.float32)],
    )(place, x, blocks)


def stage(dst, at, mine, other=None):
    for c in range(mine.shape[1] // HEAD):
        cols = slice(c * HEAD, (c + 1) * HEAD)
        block = mine[:, cols]
        if other is not None:
            block = add_pair(block, other[:, cols])
        dst[at + c] = block
    return at + mine.shape[1] // HEAD


def stage_all(chunk_refs, hg_refs, sel_ref, hg_ref):
    at = 0
    for i in range(0, len(chunk_refs), 2):
        at = stage(sel_ref, at, chunk_refs[i], chunk_refs[i + 1])
    stage(hg_ref, stage(hg_ref, 0, hg_refs[0]), hg_refs[1])


def local_grads(where, out_place, in_place, chunks, hidden_grads, attn_out, cotangent):
    tok = cotangent.shape[0]
    n_out, n_in = out_place.shape[0], in_place.shape[0]
    half_out, half_in = n_out // 2, n_in // 2
    pairs = 2 * (half_out + half_in)
    n_chunks = len(chunks)

    def kernel(where_ref, out_ref, in_ref, *refs):
        chunk_refs, refs = refs[:n_chunks], refs[n_chunks:]
        hg0, hg1, attn_ref, cot_ref, keep_ref, send_ref, sel, hg, attn, cot = refs
        stage_all(chunk_refs, (hg0, hg1), sel, hg)
        stage(attn, 0, attn_ref)
        stage(cot, 0, cot_ref)
        for which in range(2):
            core = (where_ref[0] + which) % 2
            dst = (keep_ref, send_ref)[which]
            at = 0
            for i in range(half_in):
                r = core * half_in + i
                rhs = jnp.concatenate([hg[in_ref[r, 0]], hg[in_ref[r, 1]]], 1)
                both = times(attn[r], rhs, ((0,), (0,))).astype(dst.dtype)
                for k in range(2):
                    dst[at : at + HEAD, :] = both[:, k * HEAD : (k + 1) * HEAD]
                    at += HEAD
            for i in range(half_out):
                r = core * half_out + i
                lhs = jnp.concatenate([sel[out_ref[r, 0]], sel[out_ref[r, 1]]], 1)
                dst[at : at + 2 * HEAD, :] = times(lhs, cot[r], ((0,), (0,))).astype(dst.dtype)
                at += 2 * HEAD

    def whole(x):
        return pl.BlockSpec(x.shape, lambda i, *_: (0,) * x.ndim)

    arrays = [*chunks, *hidden_grads]
    out_spec = pl.BlockSpec((pairs * HEAD, HEAD), lambda i, *_: (0, 0))
    return pl.pallas_call(
        kernel,
        grid_spec=pltpu.PrefetchScalarGridSpec(
            num_scalar_prefetch=3,
            grid=(1,),
            in_specs=[
                *[whole(x) for x in arrays],
                pl.BlockSpec((tok, n_in * HEAD), lambda i, w, *_: (0, w[1])),
                whole(cotangent),
            ],
            out_specs=[out_spec, out_spec],
            scratch_shapes=[
                pltpu.VMEM((BO_OLD, tok, HEAD), jnp.bfloat16),
                pltpu.VMEM((HG_OLD, tok, HEAD), jnp.bfloat16),
                pltpu.VMEM((n_in, tok, HEAD), jnp.bfloat16),
                pltpu.VMEM((n_out, tok, HEAD), jnp.bfloat16),
            ],
        ),
        out_shape=[
            jax.ShapeDtypeStruct((pairs * HEAD, HEAD), jnp.float32),
            jax.ShapeDtypeStruct((pairs * HEAD, HEAD), jnp.bfloat16),
        ],
    )(where, out_place, in_place, *arrays, attn_out, cotangent)


def local_outputs(where, out_place, in_place, chunks, hidden_grads, out_blocks, in_blocks):
    tok = chunks[0].shape[0]
    n_out, n_in = out_place.shape[0], in_place.shape[0]
    n_chunks = len(chunks)

    def kernel(where_ref, out_ref, in_ref, *refs):
        chunk_refs, refs = refs[:n_chunks], refs[n_chunks:]
        hg0, hg1, wo_ref, wi_ref, grown_ref, grad_ref, sel, hg = refs
        stage_all(chunk_refs, (hg0, hg1), sel, hg)
        for r in range(n_out):
            x = jnp.concatenate([sel[out_ref[r, 0]], sel[out_ref[r, 1]]], 1)
            y = times(x, wo_ref[r].reshape(2 * HEAD, HEAD), ((1,), (0,)))
            grown_ref[:, r * HEAD : (r + 1) * HEAD] = y.astype(jnp.bfloat16)
        for r in range(n_in):
            x = jnp.concatenate([hg[in_ref[r, 0]], hg[in_ref[r, 1]]], 1)
            w = jnp.concatenate([wi_ref[r, 0], wi_ref[r, 1]], 1)
            y = times(x, w, ((1,), (1,)))
            grad_ref[:, r * HEAD : (r + 1) * HEAD] = y.astype(jnp.bfloat16)

    def whole(x):
        return pl.BlockSpec(x.shape, lambda i, *_: (0,) * x.ndim)

    arrays = [*chunks, *hidden_grads]
    return pl.pallas_call(
        kernel,
        grid_spec=pltpu.PrefetchScalarGridSpec(
            num_scalar_prefetch=3,
            grid=(1,),
            in_specs=[
                *[whole(x) for x in arrays],
                whole(out_blocks),
                pl.BlockSpec((n_in, 2, HEAD, HEAD), lambda i, w, *_: (w[1], 0, 0, 0)),
            ],
            out_specs=[
                pl.BlockSpec((tok, n_out * HEAD), lambda i, *_: (0, 0)),
                pl.BlockSpec((tok, n_in * HEAD), lambda i, *_: (0, 0)),
            ],
            scratch_shapes=[
                pltpu.VMEM((BO_OLD, tok, HEAD), jnp.bfloat16),
                pltpu.VMEM((HG_OLD, tok, HEAD), jnp.bfloat16),
            ],
        ),
        out_shape=[
            jax.ShapeDtypeStruct((tok, n_out * HEAD), jnp.bfloat16),
            jax.ShapeDtypeStruct((tok, n_in * HEAD), jnp.bfloat16),
        ],
    )(where, out_place, in_place, *arrays, out_blocks, in_blocks)


def unpack_sums(where, mine, theirs, cut):
    rows = mine.shape[0]

    def kernel(where_ref, mine_ref, theirs_ref, in_ref, out_ref):
        for step, src in enumerate((mine_ref, theirs_ref)):

            @pl.when(pl.program_id(0) == step)
            def _():
                in_ref[0] = src[:cut, :].astype(jnp.float32)
                out_ref[0] = src[cut:, :].astype(jnp.float32)

    whole = pl.BlockSpec((rows, HEAD), lambda i, *_: (0, 0))
    return pl.pallas_call(
        kernel,
        grid_spec=pltpu.PrefetchScalarGridSpec(
            num_scalar_prefetch=1,
            grid=(2,),
            in_specs=[whole, whole],
            out_specs=[
                pl.BlockSpec((1, cut, HEAD), lambda i, w: ((w[0] + i) % 2, 0, 0)),
                pl.BlockSpec((1, rows - cut, HEAD), lambda i, w: ((w[0] + i) % 2, 0, 0)),
            ],
        ),
        out_shape=[
            jax.ShapeDtypeStruct((2, cut, HEAD), jnp.float32),
            jax.ShapeDtypeStruct((2, rows - cut, HEAD), jnp.float32),
        ],
    )(where, mine, theirs)


def token_sum(keep, send, scale):
    plane = ("xh", "y")
    n = lax.axis_size(plane)
    mine = (keep + swap_cores(send).astype(jnp.float32)).astype(jnp.bfloat16)
    rows = mine.shape[0]
    parts = lax.all_to_all(mine.reshape(n, rows // n, HEAD), plane, 0, 0, tiled=True)
    part = jnp.sum(parts.astype(jnp.float32), axis=0).astype(jnp.bfloat16)
    spread = jnp.broadcast_to(part[None], (lax.axis_size("z"),) + part.shape)
    parts = lax.all_to_all(spread, "z", 0, 0, tiled=True)
    part = (jnp.sum(parts.astype(jnp.float32), axis=0) * scale).astype(jnp.bfloat16)
    spread = jnp.broadcast_to(part[None], (n,) + part.shape)
    return lax.all_to_all(spread, plane, 0, 0, tiled=True).reshape(rows, HEAD)


def local(
    attn_out,
    cotangent,
    old_weights,
    depth_coef,
    depth_pick,
    in_blocks,
    in_cols,
    out_blocks,
    out_cols,
):
    tie = lax.optimization_barrier
    tok_rows = attn_out.shape[0]
    core = lax.axis_index("c")
    tensor_half = lax.axis_index("xl")
    local_old = old_weights.shape[1]
    local_blocks = local_old // HEAD
    rows_in = HG_NEW // lax.axis_size("xl")
    where = jnp.stack([core, tensor_half]).astype(jnp.int32)
    out_place = arrival_place(out_cols).astype(jnp.int32)
    own = in_cols // local_blocks == tensor_half
    hidden_place = jnp.where(own, in_cols % local_blocks, local_blocks)
    in_place = in_cols % local_blocks + jnp.where(own, 0, local_blocks)
    in_place = lax.dynamic_slice_in_dim(in_place, tensor_half * rows_in, rows_in, 0)

    mixed = jnp.zeros(old_weights.shape[1:], jnp.float32)
    for layer in range(L_OLD):
        weight = jnp.sum(jnp.where(depth_pick == layer, depth_coef, 0.0))
        mixed = mixed + weight * old_weights[layer].astype(jnp.float32)
    mixed = mixed.astype(jnp.bfloat16)

    n = lax.axis_size("z")
    up = [(i, (i + 1) % n) for i in range(n)]
    down = [(i, (i - 1) % n) for i in range(n)]

    def hop(a, b):
        return lax.ppermute(a, "z", up), lax.ppermute(b, "z", down)

    def forward_chunk(pieces):
        part = jnp.concatenate([forward(hidden, p) for p in pieces], axis=1)
        return part.astype(jnp.bfloat16)

    def backward_chunk(at, pieces):
        total = 0.0
        for i, p in enumerate(pieces):
            cols = slice((at + 2 * i) * HEAD, (at + 2 * i + 2) * HEAD)
            total = total + backward(old_grad[:, cols], p)
        return total

    a, b = hop(mixed, mixed)
    chunk0 = [mixed, swap_cores(mixed)]
    grad_part = scatter_blocks(cotangent, out_blocks, out_place, BO_OLD, BO_OLD, True)
    a, b, grad_part, attn_tied = tie((a, b, grad_part, attn_out))
    chunk1 = [a, swap_cores(a), b, swap_cores(b)]
    a, b = hop(a, b)
    grad_other = swap_halves(grad_part)
    hidden = scatter_blocks(
        attn_tied, in_blocks, hidden_place, local_blocks + 1, local_blocks, False
    )
    a, b, hidden = tie((a, b, hidden))
    chunk2 = [a, swap_cores(a), b, swap_cores(b)]
    a, b = hop(a, b)
    parts = [forward_chunk(chunk0), forward_chunk(chunk1)]
    a, b, parts[0], parts[1], hidden = tie((a, b, parts[0], parts[1], hidden))
    chunk3 = [a, swap_cores(a), b, swap_cores(b)]
    half = local_old // 2
    a, b = hop(a[:half], b[half:])
    chunk4 = [(a, b), (swap_cores(a), swap_cores(b))]
    chunks = [parts[0], swap_halves(parts[0]), parts[1], swap_halves(parts[1])]
    old_grad = add_pair(grad_part, grad_other)
    hidden_grad = 0.0
    for at, pieces in ((4, chunk1), (12, chunk2), (20, chunk3), (28, chunk4)):
        if at > 4:
            part = forward_chunk(pieces)
            chunks += [part, swap_halves(part)]
        else:
            hidden_grad = backward_chunk(0, chunk0)
        hidden_grad = hidden_grad + backward_chunk(at, pieces)
    hidden_grad = hidden_grad.astype(jnp.bfloat16)
    hidden_grads = [hidden_grad, swap_halves(hidden_grad)]
    keep, send = local_grads(
        where, out_place, in_place, chunks, hidden_grads, attn_out, cotangent
    )
    grown_out, grad_attn = local_outputs(
        where, out_place, in_place, chunks, hidden_grads, out_blocks, in_blocks
    )
    grad_scale = float(tok_rows * lax.axis_size(("xh", "y", "z", "c"))) ** (-0.5)
    full = token_sum(keep, send, grad_scale)
    in_sum, out_sum = unpack_sums(where, full, swap_cores(full), rows_in * HEAD)
    in_sum = in_sum.reshape(rows_in, 2, HEAD, HEAD)
    out_sum = out_sum.reshape(out_cols.shape[0], 2, HEAD, HEAD)
    return (grown_out, grad_attn, in_sum, out_sum)


def solution(mesh):
    fine = Mesh(mesh.devices.reshape(2, 4, 8, 2, 2), ("xh", "y", "z", "c", "xl"))
    tokens = ("xh", "y", "z", "c")
    placed = (
        P(tokens, None),
        P(tokens, "xl"),
        P(None, "xl", ("z", "c")),
        P(),
        P(),
        P(),
        P(),
        P("xl", None, None, None),
        P("xl", None),
    )
    return jax.shard_map(
        local,
        mesh=fine,
        in_specs=placed,
        out_specs=(
            P(tokens, "xl"),
            P(tokens, "xl"),
            P("xl", None, None, None),
            P("xl", None, None, None),
        ),
        check_vma=False,
    )
```

```python
import jax
import jax.numpy as jnp
from jax import lax
from jax.experimental import pallas as pl
from jax.experimental.pallas import tpu as pltpu
from jax.sharding import Mesh
from jax.sharding import PartitionSpec as P


HEAD = 128
HG_OLD = 16
HG_NEW = 20
BO_OLD = 32
PAIR = [(0, 1), (1, 0)]


def swap_cores(x):
    return lax.ppermute(x, "c", PAIR)


def swap_halves(x):
    return lax.ppermute(x, "xl", PAIR)


def add_pair(mine, other):
    return (mine.astype(jnp.float32) + other.astype(jnp.float32)).astype(jnp.bfloat16)


def arrival_place(cols):
    shard = cols // 2
    z = lax.axis_index("z")
    away = (shard // 2 - z) * (2 * (z % 2) - 1) % lax.axis_size("z")
    base = jnp.where(away < 4, 8 * away, 60 - 8 * away)
    return base + 2 * (shard % 2 != lax.axis_index("c")) + cols % 2


def forward(x, piece):
    if isinstance(piece, tuple):
        half = piece[0].shape[0]
        return forward(x[:, :half], piece[0]) + forward(x[:, half:], piece[1])
    return jnp.dot(x, piece, preferred_element_type=jnp.float32)


def backward(g, piece):
    if isinstance(piece, tuple):
        return jnp.concatenate([backward(g, part) for part in piece], axis=1)
    return lax.dot_general(
        g, piece, (((1,), (1,)), ((), ())), preferred_element_type=jnp.float32
    )


SMEM = pl.BlockSpec(memory_space=pltpu.SMEM)


def times(x, w, dims):
    return lax.dot_general(x, w, (dims, ((), ())), preferred_element_type=jnp.float32)


def scatter_blocks(x, blocks, place, slots, used, transposed):
    rows = blocks.shape[0]
    tok = x.shape[0]

    def kernel(place_ref, x_ref, w_ref, o_ref, acc_ref):
        acc_ref[...] = jnp.zeros_like(acc_ref)
        for r in range(rows):
            xr = x_ref[:, r * HEAD : (r + 1) * HEAD]
            if transposed:
                both = times(xr, w_ref[r].reshape(2 * HEAD, HEAD), ((1,), (1,)))
            else:
                both = times(xr, jnp.concatenate([w_ref[r, 0], w_ref[r, 1]], 1), ((1,), (0,)))
            for k in range(2):
                c = place_ref[r, k]
                acc_ref[c] = acc_ref[c] + both[:, k * HEAD : (k + 1) * HEAD]
        for c in range(used):
            o_ref[:, c * HEAD : (c + 1) * HEAD] = acc_ref[c].astype(jnp.bfloat16)

    full = pl.BlockSpec(memory_space=pltpu.VMEM)
    return pl.pallas_call(
        kernel,
        out_shape=jax.ShapeDtypeStruct((tok, used * HEAD), jnp.bfloat16),
        in_specs=[SMEM, full, full],
        out_specs=full,
        scratch_shapes=[pltpu.VMEM((slots, tok, HEAD), jnp.float32)],
    )(place, x, blocks)


def stage(dst, at, mine, other=None):
    for c in range(mine.shape[1] // HEAD):
        cols = slice(c * HEAD, (c + 1) * HEAD)
        block = mine[:, cols]
        if other is not None:
            block = add_pair(block, other[:, cols])
        dst[at + c] = block
    return at + mine.shape[1] // HEAD


def vmem(*shape):
    return pltpu.VMEM(shape, jnp.bfloat16)


def whole(x):
    return pl.BlockSpec(x.shape, lambda i, *_: (0,) * len(x.shape))


def width_rows(where, place, chunks, cotangent, blocks):
    tok = cotangent.shape[0]
    rows = place.shape[0]
    half = rows // 2
    n_chunks = len(chunks)

    def kernel(where_ref, place_ref, *refs):
        chunk_refs, refs = refs[:n_chunks], refs[n_chunks:]
        cot_ref, w_ref, grown_ref, keep_ref, send_ref, sel, cot = refs
        at = 0
        for i in range(0, n_chunks, 2):
            at = stage(sel, at, chunk_refs[i], chunk_refs[i + 1])
        stage(cot, 0, cot_ref)
        for which in range(2):
            core = (where_ref[0] + which) % 2
            dst = (send_ref, keep_ref)[1 - which]
            for i in range(half):
                r = core * half + i
                x = jnp.concatenate([sel[place_ref[r, 0]], sel[place_ref[r, 1]]], 1)
                at = 2 * HEAD * i
                dst[at : at + 2 * HEAD, :] = times(x, cot[r], ((0,), (0,))).astype(dst.dtype)
        for r in range(rows):
            x = jnp.concatenate([sel[place_ref[r, 0]], sel[place_ref[r, 1]]], 1)
            y = times(x, w_ref[r].reshape(2 * HEAD, HEAD), ((1,), (0,)))
            grown_ref[:, r * HEAD : (r + 1) * HEAD] = y.astype(jnp.bfloat16)

    out_shape = [
        jax.ShapeDtypeStruct((tok, rows * HEAD), jnp.bfloat16),
        jax.ShapeDtypeStruct((rows * HEAD, HEAD), jnp.float32),
        jax.ShapeDtypeStruct((rows * HEAD, HEAD), jnp.bfloat16),
    ]
    return pl.pallas_call(
        kernel,
        grid_spec=pltpu.PrefetchScalarGridSpec(
            num_scalar_prefetch=2,
            grid=(1,),
            in_specs=[whole(x) for x in (*chunks, cotangent, blocks)],
            out_specs=[whole(x) for x in out_shape],
            scratch_shapes=[vmem(BO_OLD, tok, HEAD), vmem(rows, tok, HEAD)],
        ),
        out_shape=out_shape,
    )(where, place, *chunks, cotangent, blocks)


def head_terms(where, place, hidden_grads, attn_out):
    tok = attn_out.shape[0]
    rows = place.shape[0]
    half = rows // 2

    def kernel(where_ref, place_ref, hg0, hg1, attn_ref, keep_ref, send_ref, hg, attn):
        stage(hg, stage(hg, 0, hg0), hg1)
        stage(attn, 0, attn_ref)
        for which in range(2):
            core = (where_ref[0] + which) % 2
            dst = (send_ref, keep_ref)[1 - which]
            for i in range(half):
                r = core * half + i
                rhs = jnp.concatenate([hg[place_ref[r, 0]], hg[place_ref[r, 1]]], 1)
                both = times(attn[r], rhs, ((0,), (0,))).astype(dst.dtype)
                for k in range(2):
                    at = (2 * i + k) * HEAD
                    dst[at : at + HEAD, :] = both[:, k * HEAD : (k + 1) * HEAD]

    out_shape = [
        jax.ShapeDtypeStruct((rows * HEAD, HEAD), jnp.float32),
        jax.ShapeDtypeStruct((rows * HEAD, HEAD), jnp.bfloat16),
    ]
    return pl.pallas_call(
        kernel,
        grid_spec=pltpu.PrefetchScalarGridSpec(
            num_scalar_prefetch=2,
            grid=(1,),
            in_specs=[
                *[whole(x) for x in hidden_grads],
                pl.BlockSpec((tok, rows * HEAD), lambda i, w, *_: (0, w[1])),
            ],
            out_specs=[whole(x) for x in out_shape],
            scratch_shapes=[vmem(HG_OLD, tok, HEAD), vmem(rows, tok, HEAD)],
        ),
        out_shape=out_shape,
    )(where, place, *hidden_grads, attn_out)


def head_grads(where, place, hidden_grads, blocks):
    tok = hidden_grads[0].shape[0]
    rows = place.shape[0]

    def kernel(where_ref, place_ref, hg0, hg1, w_ref, grad_ref, hg):
        stage(hg, stage(hg, 0, hg0), hg1)
        for r in range(rows):
            x = jnp.concatenate([hg[place_ref[r, 0]], hg[place_ref[r, 1]]], 1)
            w = jnp.concatenate([w_ref[r, 0], w_ref[r, 1]], 1)
            y = times(x, w, ((1,), (1,)))
            grad_ref[:, r * HEAD : (r + 1) * HEAD] = y.astype(jnp.bfloat16)

    out_shape = jax.ShapeDtypeStruct((tok, rows * HEAD), jnp.bfloat16)
    return pl.pallas_call(
        kernel,
        grid_spec=pltpu.PrefetchScalarGridSpec(
            num_scalar_prefetch=2,
            grid=(1,),
            in_specs=[
                *[whole(x) for x in hidden_grads],
                pl.BlockSpec((rows, 2, HEAD, HEAD), lambda i, w, *_: (w[1], 0, 0, 0)),
            ],
            out_specs=whole(out_shape),
            scratch_shapes=[vmem(HG_OLD, tok, HEAD)],
        ),
        out_shape=out_shape,
    )(where, place, *hidden_grads, blocks)


def mix_layers(pick, coef, weights):
    rows, cols = weights.shape[1:]
    steps = 2

    def kernel(pick_ref, coef_ref, first_ref, second_ref, o_ref):
        total = coef_ref[0] * first_ref[0].astype(jnp.float32)
        total = total + coef_ref[1] * second_ref[0].astype(jnp.float32)
        o_ref[...] = total.astype(jnp.bfloat16)

    def layer(slot):
        return pl.BlockSpec((1, rows // steps, cols), lambda i, p, c: (p[slot], i, 0))

    return pl.pallas_call(
        kernel,
        grid_spec=pltpu.PrefetchScalarGridSpec(
            num_scalar_prefetch=2,
            grid=(steps,),
            in_specs=[layer(0), layer(1)],
            out_specs=pl.BlockSpec((rows // steps, cols), lambda i, p, c: (i, 0)),
        ),
        out_shape=jax.ShapeDtypeStruct((rows, cols), jnp.bfloat16),
    )(pick, coef, weights, weights)


def unpack_sums(where, mine, theirs, cut):
    rows = mine.shape[0]

    def kernel(where_ref, mine_ref, theirs_ref, in_ref, out_ref):
        for step, src in enumerate((mine_ref, theirs_ref)):

            @pl.when(pl.program_id(0) == step)
            def _():
                in_ref[0] = src[:cut, :].astype(jnp.float32)
                out_ref[0] = src[cut:, :].astype(jnp.float32)

    return pl.pallas_call(
        kernel,
        grid_spec=pltpu.PrefetchScalarGridSpec(
            num_scalar_prefetch=1,
            grid=(2,),
            in_specs=[whole(mine), whole(theirs)],
            out_specs=[
                pl.BlockSpec((1, cut, HEAD), lambda i, w: ((w[0] + i) % 2, 0, 0)),
                pl.BlockSpec((1, rows - cut, HEAD), lambda i, w: ((w[0] + i) % 2, 0, 0)),
            ],
        ),
        out_shape=[
            jax.ShapeDtypeStruct((2, cut, HEAD), jnp.float32),
            jax.ShapeDtypeStruct((2, rows - cut, HEAD), jnp.float32),
        ],
    )(where, mine, theirs)


def token_sum(keep, came, scale):
    plane = ("xh", "y")
    n = lax.axis_size(plane)
    mine = [(k + c.astype(jnp.float32)).astype(jnp.bfloat16) for k, c in zip(keep, came)]
    mine = jnp.concatenate(mine, axis=0)
    rows = mine.shape[0]
    parts = lax.all_to_all(mine.reshape(n, rows // n, HEAD), plane, 0, 0, tiled=True)
    part = jnp.sum(parts.astype(jnp.float32), axis=0).astype(jnp.bfloat16)
    spread = jnp.broadcast_to(part[None], (lax.axis_size("z"),) + part.shape)
    parts = lax.all_to_all(spread, "z", 0, 0, tiled=True)
    part = (jnp.sum(parts.astype(jnp.float32), axis=0) * scale).astype(jnp.bfloat16)
    spread = jnp.broadcast_to(part[None], (n,) + part.shape)
    return lax.all_to_all(spread, plane, 0, 0, tiled=True).reshape(rows, HEAD)


def local(
    attn_out,
    cotangent,
    old_weights,
    depth_coef,
    depth_pick,
    in_blocks,
    in_cols,
    out_blocks,
    out_cols,
):
    tok_rows = attn_out.shape[0]
    core = lax.axis_index("c")
    tensor_half = lax.axis_index("xl")
    local_old = old_weights.shape[1]
    local_blocks = local_old // HEAD
    rows_in = HG_NEW // lax.axis_size("xl")
    where = jnp.stack([core, tensor_half]).astype(jnp.int32)
    out_place = arrival_place(out_cols).astype(jnp.int32)
    own = in_cols // local_blocks == tensor_half
    hidden_place = jnp.where(own, in_cols % local_blocks, local_blocks)
    in_place = in_cols % local_blocks + jnp.where(own, 0, local_blocks)
    in_place = lax.dynamic_slice_in_dim(in_place, tensor_half * rows_in, rows_in, 0)

    n = lax.axis_size("z")
    even = [(i, i ^ 1) for i in range(n)]
    odd = [(i, (i - 1 + 2 * (i % 2)) % n) for i in range(n)]

    def hop(a, b):
        return lax.ppermute(b, "z", even), lax.ppermute(a, "z", odd)

    def cores(*pieces):
        return [q for p in pieces for q in (p, swap_cores(p))]

    def forward_chunk(pieces):
        part = jnp.concatenate([forward(hidden, p) for p in pieces], axis=1)
        part = part.astype(jnp.bfloat16)
        return [part, swap_halves(part)]

    def backward_chunk(at, pieces, total):
        for p in pieces:
            total = total + backward(old_grad[:, at * HEAD : (at + 2) * HEAD], p)
            at += 2
        return total

    grad_part = scatter_blocks(cotangent, out_blocks, out_place, BO_OLD, BO_OLD, True)
    grad_other = swap_halves(grad_part)
    mixed = mix_layers(depth_pick, depth_coef, old_weights)
    chunk0 = cores(mixed)
    a, b = hop(mixed, mixed)
    hidden = scatter_blocks(
        attn_out, in_blocks, hidden_place, local_blocks + 1, local_blocks, False
    )
    parts = forward_chunk(chunk0)
    chunk1 = cores(a, b)
    a, b = hop(a, b)
    parts += forward_chunk(chunk1)
    chunk2 = cores(a, b)
    a, b = hop(a, b)
    parts += forward_chunk(chunk2)
    old_grad = add_pair(grad_part, grad_other)
    hidden_grad = backward_chunk(0, chunk0, 0.0)
    hidden_grad = backward_chunk(4, chunk1, hidden_grad)
    chunk3 = cores(a, b)
    half = local_old // 2
    a, b = hop(a[half:], b[:half])
    chunk4 = [(a, b), (swap_cores(a), swap_cores(b))]
    parts += forward_chunk(chunk3)
    hidden_grad = backward_chunk(12, chunk2, hidden_grad)
    hidden_grad = backward_chunk(20, chunk3, hidden_grad)
    parts += forward_chunk(chunk4)
    hidden_grad = backward_chunk(28, chunk4, hidden_grad).astype(jnp.bfloat16)
    hidden_grads = [hidden_grad, swap_halves(hidden_grad)]
    grown_out, keep_out, send_out = width_rows(
        where, out_place, parts, cotangent, out_blocks
    )
    came_out = swap_cores(send_out)
    keep_in, send_in = head_terms(where, in_place, hidden_grads, attn_out)
    came_in = swap_cores(send_in)
    grad_attn = head_grads(where, in_place, hidden_grads, in_blocks)
    grad_scale = float(tok_rows * lax.axis_size(("xh", "y", "z", "c"))) ** (-0.5)
    full = token_sum((keep_in, keep_out), (came_in, came_out), grad_scale)
    theirs = swap_cores(full)
    in_sum, out_sum = unpack_sums(where, full, theirs, rows_in * HEAD)
    in_sum = in_sum.reshape(rows_in, 2, HEAD, HEAD)
    out_sum = out_sum.reshape(out_cols.shape[0], 2, HEAD, HEAD)
    return (grown_out, grad_attn, in_sum, out_sum)


def solution(mesh):
    fine = Mesh(mesh.devices.reshape(2, 4, 8, 2, 2), ("xh", "y", "z", "c", "xl"))
    tokens = ("xh", "y", "z", "c")
    placed = (
        P(tokens, None),
        P(tokens, "xl"),
        P(None, "xl", ("z", "c")),
        P(),
        P(),
        P(),
        P(),
        P("xl", None, None, None),
        P("xl", None),
    )
    return jax.shard_map(
        local,
        mesh=fine,
        in_specs=placed,
        out_specs=(
            P(tokens, "xl"),
            P(tokens, "xl"),
            P("xl", None, None, None),
            P("xl", None, None, None),
        ),
        check_vma=False,
    )
```

```python
import jax
import jax.numpy as jnp
from jax import lax
from jax.experimental import pallas as pl
from jax.experimental.pallas import tpu as pltpu
from jax.sharding import Mesh
from jax.sharding import PartitionSpec as P


HEAD = 128
HG_OLD = 16
HG_NEW = 20
BO_OLD = 32
PAIR = [(0, 1), (1, 0)]
Z = ("zh", "zl")
TOKENS = ("xh", "y", *Z, "c")


def swap_cores(x):
    return lax.ppermute(x, "c", PAIR)


def swap_halves(x):
    return lax.ppermute(x, "xl", PAIR)


def add_pair(mine, other):
    return (mine.astype(jnp.float32) + other.astype(jnp.float32)).astype(jnp.bfloat16)


def arrival_place(cols):
    shard = cols // 2
    z = lax.axis_index(Z)
    away = (shard // 2 - z) * (2 * (z % 2) - 1) % lax.axis_size(Z)
    base = jnp.where(away < 4, 8 * away, 60 - 8 * away)
    return base + 2 * (shard % 2 != lax.axis_index("c")) + cols % 2


def forward(x, piece):
    if isinstance(piece, tuple):
        half = piece[0].shape[0]
        return forward(x[:, :half], piece[0]) + forward(x[:, half:], piece[1])
    return jnp.dot(x, piece, preferred_element_type=jnp.float32)


def backward(g, piece):
    if isinstance(piece, tuple):
        return jnp.concatenate([backward(g, part) for part in piece], axis=1)
    return lax.dot_general(
        g, piece, (((1,), (1,)), ((), ())), preferred_element_type=jnp.float32
    )


HERE = pl.BlockSpec(memory_space=pltpu.VMEM)
VMEM = pltpu.VMEM
SMEM = pl.BlockSpec(memory_space=pltpu.SMEM)


def grant(mib):
    return pltpu.CompilerParams(vmem_limit_bytes=mib << 20)


def near(x):
    return pltpu.with_memory_space_constraint(x, VMEM)


def times(x, w, dims):
    return lax.dot_general(x, w, (dims, ((), ())), preferred_element_type=jnp.float32)


def scatter_blocks(x, blocks, place, slots, used, transposed):
    rows = blocks.shape[0]
    tok = x.shape[0]

    def kernel(place_ref, x_ref, w_ref, o_ref, acc_ref):
        acc_ref[...] = jnp.zeros_like(acc_ref)
        for r in range(rows):
            xr = x_ref[:, r * HEAD : (r + 1) * HEAD]
            if transposed:
                both = times(xr, w_ref[r].reshape(2 * HEAD, HEAD), ((1,), (1,)))
            else:
                both = times(xr, jnp.concatenate([w_ref[r, 0], w_ref[r, 1]], 1), ((1,), (0,)))
            for k in range(2):
                c = place_ref[r, k]
                acc_ref[c] = acc_ref[c] + both[:, k * HEAD : (k + 1) * HEAD]
        for c in range(used):
            o_ref[:, c * HEAD : (c + 1) * HEAD] = acc_ref[c].astype(jnp.bfloat16)

    full = pl.BlockSpec(memory_space=pltpu.VMEM)
    return pl.pallas_call(
        kernel,
        out_shape=VMEM((tok, used * HEAD), jnp.bfloat16),
        in_specs=[SMEM, full, full],
        out_specs=full,
        scratch_shapes=[pltpu.VMEM((slots, tok, HEAD), jnp.float32)],
        compiler_params=grant(16),
    )(place, x, blocks)


def stage(dst, at, mine, other=None):
    for c in range(mine.shape[1] // HEAD):
        cols = slice(c * HEAD, (c + 1) * HEAD)
        block = mine[:, cols]
        if other is not None:
            block = add_pair(block, other[:, cols])
        dst[at + c] = block
    return at + mine.shape[1] // HEAD


def vmem(*shape):
    return pltpu.VMEM(shape, jnp.bfloat16)


def whole(x):
    return pl.BlockSpec(x.shape, lambda i, *_: (0,) * len(x.shape))


def width_rows(where, place, chunks, cotangent, blocks):
    tok = cotangent.shape[0]
    rows = place.shape[0]
    half = rows // 2
    n_chunks = len(chunks)

    def kernel(where_ref, place_ref, *refs):
        chunk_refs, refs = refs[:n_chunks], refs[n_chunks:]
        cot_ref, w_ref, grown_ref, keep_ref, send_ref, sel, cot = refs
        at = 0
        for i in range(0, n_chunks, 2):
            at = stage(sel, at, chunk_refs[i], chunk_refs[i + 1])
        stage(cot, 0, cot_ref)
        for which in range(2):
            core = (where_ref[0] + which) % 2
            dst = (send_ref, keep_ref)[1 - which]
            for i in range(half):
                r = core * half + i
                x = jnp.concatenate([sel[place_ref[r, 0]], sel[place_ref[r, 1]]], 1)
                at = 2 * HEAD * i
                dst[at : at + 2 * HEAD, :] = times(x, cot[r], ((0,), (0,))).astype(dst.dtype)
        for r in range(rows):
            x = jnp.concatenate([sel[place_ref[r, 0]], sel[place_ref[r, 1]]], 1)
            y = times(x, w_ref[r].reshape(2 * HEAD, HEAD), ((1,), (0,)))
            grown_ref[:, r * HEAD : (r + 1) * HEAD] = y.astype(jnp.bfloat16)

    out_shape = [
        jax.ShapeDtypeStruct((tok, rows * HEAD), jnp.bfloat16),
        VMEM((rows * HEAD, HEAD), jnp.float32),
        VMEM((rows * HEAD, HEAD), jnp.bfloat16),
    ]
    return pl.pallas_call(
        kernel,
        grid_spec=pltpu.PrefetchScalarGridSpec(
            num_scalar_prefetch=2,
            grid=(1,),
            in_specs=[*[HERE for _ in chunks], whole(cotangent), whole(blocks)],
            out_specs=[whole(out_shape[0]), HERE, HERE],
            scratch_shapes=[vmem(BO_OLD, tok, HEAD), vmem(rows, tok, HEAD)],
        ),
        out_shape=out_shape,
        compiler_params=grant(20),
    )(where, place, *map(near, chunks), cotangent, blocks)


def head_terms(where, place, hidden_grads, attn_out):
    tok = attn_out.shape[0]
    rows = place.shape[0]
    half = rows // 2

    def kernel(where_ref, place_ref, hg0, hg1, attn_ref, keep_ref, send_ref, hg, attn):
        stage(hg, stage(hg, 0, hg0), hg1)
        stage(attn, 0, attn_ref)
        for which in range(2):
            core = (where_ref[0] + which) % 2
            dst = (send_ref, keep_ref)[1 - which]
            for i in range(half):
                r = core * half + i
                rhs = jnp.concatenate([hg[place_ref[r, 0]], hg[place_ref[r, 1]]], 1)
                both = times(attn[r], rhs, ((0,), (0,))).astype(dst.dtype)
                for k in range(2):
                    at = (2 * i + k) * HEAD
                    dst[at : at + HEAD, :] = both[:, k * HEAD : (k + 1) * HEAD]

    out_shape = [
        VMEM((rows * HEAD, HEAD), jnp.float32),
        VMEM((rows * HEAD, HEAD), jnp.bfloat16),
    ]
    return pl.pallas_call(
        kernel,
        grid_spec=pltpu.PrefetchScalarGridSpec(
            num_scalar_prefetch=2,
            grid=(1,),
            in_specs=[
                *[HERE for _ in hidden_grads],
                pl.BlockSpec((tok, rows * HEAD), lambda i, w, *_: (0, w[1])),
            ],
            out_specs=[HERE, HERE],
            scratch_shapes=[vmem(HG_OLD, tok, HEAD), vmem(rows, tok, HEAD)],
        ),
        out_shape=out_shape,
        compiler_params=grant(12),
    )(where, place, *map(near, hidden_grads), attn_out)


def head_grads(where, place, hidden_grads, blocks):
    tok = hidden_grads[0].shape[0]
    rows = place.shape[0]

    def kernel(where_ref, place_ref, hg0, hg1, w_ref, grad_ref, hg):
        stage(hg, stage(hg, 0, hg0), hg1)
        for r in range(rows):
            x = jnp.concatenate([hg[place_ref[r, 0]], hg[place_ref[r, 1]]], 1)
            w = jnp.concatenate([w_ref[r, 0], w_ref[r, 1]], 1)
            y = times(x, w, ((1,), (1,)))
            grad_ref[:, r * HEAD : (r + 1) * HEAD] = y.astype(jnp.bfloat16)

    out_shape = jax.ShapeDtypeStruct((tok, rows * HEAD), jnp.bfloat16)
    return pl.pallas_call(
        kernel,
        grid_spec=pltpu.PrefetchScalarGridSpec(
            num_scalar_prefetch=2,
            grid=(1,),
            in_specs=[
                *[HERE for _ in hidden_grads],
                pl.BlockSpec((rows, 2, HEAD, HEAD), lambda i, w, *_: (w[1], 0, 0, 0)),
            ],
            out_specs=whole(out_shape),
            scratch_shapes=[vmem(HG_OLD, tok, HEAD)],
        ),
        out_shape=out_shape,
        compiler_params=grant(12),
    )(where, place, *map(near, hidden_grads), blocks)


def mix_layers(pick, coef, weights):
    rows, cols = weights.shape[1:]
    steps = 2

    def kernel(pick_ref, coef_ref, first_ref, second_ref, o_ref):
        total = coef_ref[0] * first_ref[0].astype(jnp.float32)
        total = total + coef_ref[1] * second_ref[0].astype(jnp.float32)
        at = pl.multiple_of(pl.program_id(0) * (rows // steps), rows // steps)
        o_ref[pl.ds(at, rows // steps), :] = total.astype(jnp.bfloat16)

    def layer(slot):
        return pl.BlockSpec((1, rows // steps, cols), lambda i, p, c: (p[slot], i, 0))

    return pl.pallas_call(
        kernel,
        grid_spec=pltpu.PrefetchScalarGridSpec(
            num_scalar_prefetch=2,
            grid=(steps,),
            in_specs=[layer(0), layer(1)],
            out_specs=HERE,
        ),
        out_shape=VMEM((rows, cols), jnp.bfloat16),
        compiler_params=grant(6),
    )(pick, coef, weights, weights)


def unpack_sums(where, mine, theirs, cut):
    steps = 2
    most = mine.shape[0] - cut
    small, large = cut // steps, most // steps

    def kernel(where_ref, mine_ref, theirs_ref, in_ref, out_ref):
        i = pl.program_id(1)
        for turn, src in enumerate((mine_ref, theirs_ref)):

            @pl.when(pl.program_id(0) == turn)
            def _():
                at = pl.multiple_of(i * small, small)
                in_ref[0] = src[pl.ds(at, small), :].astype(jnp.float32)
                at = pl.multiple_of(cut + i * large, small)
                out_ref[0] = src[pl.ds(at, large), :].astype(jnp.float32)

    def result(rows):
        return pl.BlockSpec((1, rows, HEAD), lambda t, i, w: ((w[0] + t) % 2, i, 0))

    return pl.pallas_call(
        kernel,
        grid_spec=pltpu.PrefetchScalarGridSpec(
            num_scalar_prefetch=1,
            grid=(2, steps),
            in_specs=[HERE, HERE],
            out_specs=[result(small), result(large)],
        ),
        out_shape=[
            jax.ShapeDtypeStruct((2, cut, HEAD), jnp.float32),
            jax.ShapeDtypeStruct((2, most, HEAD), jnp.float32),
        ],
        compiler_params=grant(14),
    )(where, near(mine), near(theirs))


def token_sum(keep, came, scale):
    plane = ("xh", "y", "zl")
    n = lax.axis_size(plane)
    mine = [(k + c.astype(jnp.float32)).astype(jnp.bfloat16) for k, c in zip(keep, came)]
    mine = jnp.concatenate(mine, axis=0)
    rows = mine.shape[0]
    parts = lax.all_to_all(mine.reshape(n, rows // n, HEAD), plane, 0, 0, tiled=True)
    part = jnp.sum(parts.astype(jnp.float32), axis=0).astype(jnp.bfloat16)
    spread = jnp.broadcast_to(part[None], (lax.axis_size("zh"),) + part.shape)
    parts = lax.all_to_all(spread, "zh", 0, 0, tiled=True)
    part = (jnp.sum(parts.astype(jnp.float32), axis=0) * scale).astype(jnp.bfloat16)
    spread = jnp.broadcast_to(part[None], (n,) + part.shape)
    return lax.all_to_all(spread, plane, 0, 0, tiled=True).reshape(rows, HEAD)


def local(
    attn_out,
    cotangent,
    old_weights,
    depth_coef,
    depth_pick,
    in_blocks,
    in_cols,
    out_blocks,
    out_cols,
):
    tok_rows = attn_out.shape[0]
    core = lax.axis_index("c")
    tensor_half = lax.axis_index("xl")
    local_old = old_weights.shape[1]
    local_blocks = local_old // HEAD
    rows_in = HG_NEW // lax.axis_size("xl")
    where = jnp.stack([core, tensor_half]).astype(jnp.int32)
    out_place = arrival_place(out_cols).astype(jnp.int32)
    own = in_cols // local_blocks == tensor_half
    hidden_place = jnp.where(own, in_cols % local_blocks, local_blocks)
    my_cols = lax.dynamic_slice_in_dim(in_cols, tensor_half * rows_in, rows_in, 0)
    away = my_cols // local_blocks != tensor_half
    in_place = my_cols % local_blocks + jnp.where(away, local_blocks, 0)

    n = lax.axis_size(Z)
    even = [(i, i ^ 1) for i in range(n)]
    odd = [(i, (i - 1 + 2 * (i % 2)) % n) for i in range(n)]

    def hop(a, b):
        return lax.ppermute(b, Z, even), lax.ppermute(a, Z, odd)

    def cores(*pieces):
        return [q for p in pieces for q in (p, swap_cores(p))]

    def forward_chunk(pieces):
        part = jnp.concatenate([forward(hidden, p) for p in pieces], axis=1)
        part = part.astype(jnp.bfloat16)
        return [part, swap_halves(part)]

    def backward_chunk(at, pieces, total):
        for p in pieces:
            total = total + backward(old_grad[:, at * HEAD : (at + 2) * HEAD], p)
            at += 2
        return total

    mixed = mix_layers(depth_pick, depth_coef, old_weights)
    chunk0 = cores(mixed)
    a, b = hop(mixed, mixed)
    grad_part = scatter_blocks(cotangent, out_blocks, out_place, BO_OLD, BO_OLD, True)
    grad_other = swap_halves(grad_part)
    hidden = scatter_blocks(
        attn_out, in_blocks, hidden_place, local_blocks + 1, local_blocks, False
    )
    parts = forward_chunk(chunk0)
    chunk1 = cores(a, b)
    a, b = hop(a, b)
    parts += forward_chunk(chunk1)
    chunk2 = cores(a, b)
    a, b = hop(a, b)
    parts += forward_chunk(chunk2)
    old_grad = add_pair(grad_part, grad_other)
    hidden_grad = backward_chunk(0, chunk0, 0.0)
    hidden_grad = backward_chunk(4, chunk1, hidden_grad)
    chunk3 = cores(a, b)
    half = local_old // 2
    a, b = hop(a[half:], b[:half])
    chunk4 = [(a, b), (swap_cores(a), swap_cores(b))]
    parts += forward_chunk(chunk3)
    hidden_grad = backward_chunk(12, chunk2, hidden_grad)
    hidden_grad = backward_chunk(20, chunk3, hidden_grad)
    parts += forward_chunk(chunk4)
    hidden_grad = backward_chunk(28, chunk4, hidden_grad).astype(jnp.bfloat16)
    hidden_grads = [hidden_grad, swap_halves(hidden_grad)]
    grown_out, keep_out, send_out = width_rows(
        where, out_place, parts, cotangent, out_blocks
    )
    came_out = swap_cores(send_out)
    keep_in, send_in = head_terms(where, in_place, hidden_grads, attn_out)
    came_in = swap_cores(send_in)
    grad_attn = head_grads(where, in_place, hidden_grads, in_blocks)
    grad_scale = float(tok_rows * lax.axis_size(TOKENS)) ** (-0.5)
    full = token_sum((keep_in, keep_out), (came_in, came_out), grad_scale)
    theirs = swap_cores(full)
    in_sum, out_sum = unpack_sums(where, full, theirs, rows_in * HEAD)
    in_sum = in_sum.reshape(rows_in, 2, HEAD, HEAD)
    out_sum = out_sum.reshape(out_cols.shape[0], 2, HEAD, HEAD)
    return (grown_out, grad_attn, in_sum, out_sum)


def solution(mesh):
    fine = Mesh(mesh.devices.reshape(2, 4, 4, 2, 2, 2), (*TOKENS, "xl"))
    placed = (
        P(TOKENS, None),
        P(TOKENS, "xl"),
        P(None, "xl", (*Z, "c")),
        P(),
        P(),
        P(),
        P(),
        P("xl", None, None, None),
        P("xl", None),
    )
    return jax.shard_map(
        local,
        mesh=fine,
        in_specs=placed,
        out_specs=(
            P(TOKENS, "xl"),
            P(TOKENS, "xl"),
            P("xl", None, None, None),
            P("xl", None, None, None),
        ),
        check_vma=False,
    )
```

```python
import jax
import jax.numpy as jnp
from jax import lax
from jax.experimental import pallas as pl
from jax.experimental.pallas import tpu as pltpu
from jax.sharding import Mesh
from jax.sharding import PartitionSpec as P


HEAD = 128
HG_OLD = 16
HG_NEW = 20
BO_OLD = 32
PAIR = [(0, 1), (1, 0)]
Z = ("zh", "zl")
TOKENS = ("xh", "y", *Z, "c")


def swap_cores(x):
    return lax.ppermute(x, "c", PAIR)


def swap_halves(x):
    return lax.ppermute(x, "xl", PAIR)


def add_pair(mine, other):
    return (mine.astype(jnp.float32) + other.astype(jnp.float32)).astype(jnp.bfloat16)


def arrival_place(cols):
    shard = cols // 2
    z = lax.axis_index(Z)
    away = (shard // 2 - z) * (2 * (z % 2) - 1) % lax.axis_size(Z)
    base = jnp.where(away < 4, 8 * away, 60 - 8 * away)
    return base + 2 * (shard % 2 != lax.axis_index("c")) + cols % 2


def forward(x, piece):
    if isinstance(piece, tuple):
        half = piece[0].shape[0]
        return forward(x[:, :half], piece[0]) + forward(x[:, half:], piece[1])
    return jnp.dot(x, piece, preferred_element_type=jnp.float32)


def backward(g, piece):
    if isinstance(piece, tuple):
        return jnp.concatenate([backward(g, part) for part in piece], axis=1)
    return lax.dot_general(
        g, piece, (((1,), (1,)), ((), ())), preferred_element_type=jnp.float32
    )


HERE = pl.BlockSpec(memory_space=pltpu.VMEM)
VMEM = pltpu.VMEM
SMEM = pl.BlockSpec(memory_space=pltpu.SMEM)


def grant(mib):
    return pltpu.CompilerParams(vmem_limit_bytes=mib << 20)


def near(x):
    return pltpu.with_memory_space_constraint(x, VMEM)


def times(x, w, dims):
    return lax.dot_general(x, w, (dims, ((), ())), preferred_element_type=jnp.float32)


def scatter_blocks(x, blocks, place, slots, used, transposed):
    rows = blocks.shape[0]
    tok = x.shape[0]

    def kernel(place_ref, x_ref, w_ref, o_ref, acc_ref):
        acc_ref[...] = jnp.zeros_like(acc_ref)
        for r in range(rows):
            xr = x_ref[:, r * HEAD : (r + 1) * HEAD]
            if transposed:
                both = times(xr, w_ref[r].reshape(2 * HEAD, HEAD), ((1,), (1,)))
            else:
                both = times(xr, jnp.concatenate([w_ref[r, 0], w_ref[r, 1]], 1), ((1,), (0,)))
            for k in range(2):
                c = place_ref[r, k]
                acc_ref[c] = acc_ref[c] + both[:, k * HEAD : (k + 1) * HEAD]
        for c in range(used):
            o_ref[:, c * HEAD : (c + 1) * HEAD] = acc_ref[c].astype(jnp.bfloat16)

    full = pl.BlockSpec(memory_space=pltpu.VMEM)
    return pl.pallas_call(
        kernel,
        out_shape=VMEM((tok, used * HEAD), jnp.bfloat16),
        in_specs=[SMEM, full, full],
        out_specs=full,
        scratch_shapes=[pltpu.VMEM((slots, tok, HEAD), jnp.float32)],
        compiler_params=grant(16),
    )(place, x, blocks)


def stage(dst, at, mine, other=None):
    for c in range(mine.shape[1] // HEAD):
        cols = slice(c * HEAD, (c + 1) * HEAD)
        block = mine[:, cols]
        if other is not None:
            block = add_pair(block, other[:, cols])
        dst[at + c] = block
    return at + mine.shape[1] // HEAD


def vmem(*shape):
    return pltpu.VMEM(shape, jnp.bfloat16)


def whole(x):
    return pl.BlockSpec(x.shape, lambda i, *_: (0,) * len(x.shape))


def width_rows(where, place, chunks, cotangent, blocks):
    tok = cotangent.shape[0]
    rows = place.shape[0]
    half = rows // 2
    n_chunks = len(chunks)

    def kernel(where_ref, place_ref, *refs):
        chunk_refs, refs = refs[:n_chunks], refs[n_chunks:]
        cot_ref, w_ref, grown_ref, keep_ref, send_ref, sel, cot = refs
        at = 0
        for i in range(0, n_chunks, 2):
            at = stage(sel, at, chunk_refs[i], chunk_refs[i + 1])
        stage(cot, 0, cot_ref)
        for which in range(2):
            core = (where_ref[0] + which) % 2
            dst = (send_ref, keep_ref)[1 - which]
            for i in range(half):
                r = core * half + i
                x = jnp.concatenate([sel[place_ref[r, 0]], sel[place_ref[r, 1]]], 1)
                at = 2 * HEAD * i
                dst[at : at + 2 * HEAD, :] = times(x, cot[r], ((0,), (0,))).astype(dst.dtype)
        for r in range(rows):
            x = jnp.concatenate([sel[place_ref[r, 0]], sel[place_ref[r, 1]]], 1)
            y = times(x, w_ref[r].reshape(2 * HEAD, HEAD), ((1,), (0,)))
            grown_ref[:, r * HEAD : (r + 1) * HEAD] = y.astype(jnp.bfloat16)

    out_shape = [
        jax.ShapeDtypeStruct((tok, rows * HEAD), jnp.bfloat16),
        VMEM((rows * HEAD, HEAD), jnp.float32),
        VMEM((rows * HEAD, HEAD), jnp.bfloat16),
    ]
    return pl.pallas_call(
        kernel,
        grid_spec=pltpu.PrefetchScalarGridSpec(
            num_scalar_prefetch=2,
            grid=(1,),
            in_specs=[*[HERE for _ in chunks], whole(cotangent), whole(blocks)],
            out_specs=[whole(out_shape[0]), HERE, HERE],
            scratch_shapes=[vmem(BO_OLD, tok, HEAD), vmem(rows, tok, HEAD)],
        ),
        out_shape=out_shape,
        compiler_params=grant(20),
    )(where, place, *map(near, chunks), cotangent, blocks)


def head_terms(where, place, hidden_grads, attn_out):
    tok = attn_out.shape[0]
    rows = place.shape[0]
    half = rows // 2

    def kernel(where_ref, place_ref, hg0, hg1, attn_ref, keep_ref, send_ref, hg, attn):
        stage(hg, stage(hg, 0, hg0), hg1)
        stage(attn, 0, attn_ref)
        for which in range(2):
            core = (where_ref[0] + which) % 2
            dst = (send_ref, keep_ref)[1 - which]
            for i in range(half):
                r = core * half + i
                rhs = jnp.concatenate([hg[place_ref[r, 0]], hg[place_ref[r, 1]]], 1)
                both = times(attn[r], rhs, ((0,), (0,))).astype(dst.dtype)
                for k in range(2):
                    at = (2 * i + k) * HEAD
                    dst[at : at + HEAD, :] = both[:, k * HEAD : (k + 1) * HEAD]

    out_shape = [
        VMEM((rows * HEAD, HEAD), jnp.float32),
        VMEM((rows * HEAD, HEAD), jnp.bfloat16),
    ]
    return pl.pallas_call(
        kernel,
        grid_spec=pltpu.PrefetchScalarGridSpec(
            num_scalar_prefetch=2,
            grid=(1,),
            in_specs=[
                *[HERE for _ in hidden_grads],
                pl.BlockSpec((tok, rows * HEAD), lambda i, w, *_: (0, w[1])),
            ],
            out_specs=[HERE, HERE],
            scratch_shapes=[vmem(HG_OLD, tok, HEAD), vmem(rows, tok, HEAD)],
        ),
        out_shape=out_shape,
        compiler_params=grant(12),
    )(where, place, *map(near, hidden_grads), attn_out)


def head_grads(where, place, hidden_grads, blocks):
    tok = hidden_grads[0].shape[0]
    rows = place.shape[0]

    def kernel(where_ref, place_ref, hg0, hg1, w_ref, grad_ref, hg):
        stage(hg, stage(hg, 0, hg0), hg1)
        for r in range(rows):
            x = jnp.concatenate([hg[place_ref[r, 0]], hg[place_ref[r, 1]]], 1)
            w = jnp.concatenate([w_ref[r, 0], w_ref[r, 1]], 1)
            y = times(x, w, ((1,), (1,)))
            grad_ref[:, r * HEAD : (r + 1) * HEAD] = y.astype(jnp.bfloat16)

    out_shape = jax.ShapeDtypeStruct((tok, rows * HEAD), jnp.bfloat16)
    return pl.pallas_call(
        kernel,
        grid_spec=pltpu.PrefetchScalarGridSpec(
            num_scalar_prefetch=2,
            grid=(1,),
            in_specs=[
                *[HERE for _ in hidden_grads],
                pl.BlockSpec((rows, 2, HEAD, HEAD), lambda i, w, *_: (w[1], 0, 0, 0)),
            ],
            out_specs=whole(out_shape),
            scratch_shapes=[vmem(HG_OLD, tok, HEAD)],
        ),
        out_shape=out_shape,
        compiler_params=grant(12),
    )(where, place, *map(near, hidden_grads), blocks)


def mix_layers(pick, coef, weights):
    rows, cols = weights.shape[1:]
    steps = 2

    def kernel(pick_ref, coef_ref, first_ref, second_ref, o_ref):
        total = coef_ref[0] * first_ref[0].astype(jnp.float32)
        total = total + coef_ref[1] * second_ref[0].astype(jnp.float32)
        at = pl.multiple_of(pl.program_id(0) * (rows // steps), rows // steps)
        o_ref[pl.ds(at, rows // steps), :] = total.astype(jnp.bfloat16)

    def layer(slot):
        return pl.BlockSpec((1, rows // steps, cols), lambda i, p, c: (p[slot], i, 0))

    return pl.pallas_call(
        kernel,
        grid_spec=pltpu.PrefetchScalarGridSpec(
            num_scalar_prefetch=2,
            grid=(steps,),
            in_specs=[layer(0), layer(1)],
            out_specs=HERE,
        ),
        out_shape=VMEM((rows, cols), jnp.bfloat16),
        compiler_params=grant(6),
    )(pick, coef, weights, weights)


def unpack_half(where, turn, half, cut, so_far=()):
    steps = 2
    most = half.shape[0] - cut
    small, large = cut // steps, most // steps

    def kernel(where_ref, half_ref, *refs):
        in_ref, out_ref = refs[-2:]
        i = pl.program_id(0)
        at = pl.multiple_of(i * small, small)
        in_ref[0] = half_ref[pl.ds(at, small), :].astype(jnp.float32)
        at = pl.multiple_of(cut + i * large, small)
        out_ref[0] = half_ref[pl.ds(at, large), :].astype(jnp.float32)

    def result(rows):
        return pl.BlockSpec((1, rows, HEAD), lambda i, w: ((w[0] + turn) % 2, i, 0))

    return pl.pallas_call(
        kernel,
        grid_spec=pltpu.PrefetchScalarGridSpec(
            num_scalar_prefetch=1,
            grid=(steps,),
            in_specs=[HERE, *[pl.BlockSpec(memory_space=pl.ANY) for _ in so_far]],
            out_specs=[result(small), result(large)],
        ),
        out_shape=[
            jax.ShapeDtypeStruct((2, cut, HEAD), jnp.float32),
            jax.ShapeDtypeStruct((2, most, HEAD), jnp.float32),
        ],
        input_output_aliases={2 + i: i for i in range(len(so_far))},
        compiler_params=grant(14),
    )(where, near(half), *so_far)


def token_sum(keep, came, scale):
    plane = ("xh", "y", "zl")
    n = lax.axis_size(plane)
    mine = [(k + c.astype(jnp.float32)).astype(jnp.bfloat16) for k, c in zip(keep, came)]
    mine = jnp.concatenate(mine, axis=0)
    rows = mine.shape[0]
    parts = lax.all_to_all(mine.reshape(n, rows // n, HEAD), plane, 0, 0, tiled=True)
    part = jnp.sum(parts.astype(jnp.float32), axis=0).astype(jnp.bfloat16)
    spread = jnp.broadcast_to(part[None], (lax.axis_size("zh"),) + part.shape)
    parts = lax.all_to_all(spread, "zh", 0, 0, tiled=True)
    part = (jnp.sum(parts.astype(jnp.float32), axis=0) * scale).astype(jnp.bfloat16)
    spread = jnp.broadcast_to(part[None], (n,) + part.shape)
    return lax.all_to_all(spread, plane, 0, 0, tiled=True).reshape(rows, HEAD)


def local(
    attn_out,
    cotangent,
    old_weights,
    depth_coef,
    depth_pick,
    in_blocks,
    in_cols,
    out_blocks,
    out_cols,
):
    tok_rows = attn_out.shape[0]
    core = lax.axis_index("c")
    tensor_half = lax.axis_index("xl")
    local_old = old_weights.shape[1]
    local_blocks = local_old // HEAD
    rows_in = HG_NEW // lax.axis_size("xl")
    where = jnp.stack([core, tensor_half]).astype(jnp.int32)
    out_place = arrival_place(out_cols).astype(jnp.int32)
    own = in_cols // local_blocks == tensor_half
    hidden_place = jnp.where(own, in_cols % local_blocks, local_blocks)
    my_cols = lax.dynamic_slice_in_dim(in_cols, tensor_half * rows_in, rows_in, 0)
    away = my_cols // local_blocks != tensor_half
    in_place = my_cols % local_blocks + jnp.where(away, local_blocks, 0)

    n = lax.axis_size(Z)
    even = [(i, i ^ 1) for i in range(n)]
    odd = [(i, (i - 1 + 2 * (i % 2)) % n) for i in range(n)]

    def hop(a, b):
        return lax.ppermute(b, Z, even), lax.ppermute(a, Z, odd)

    def cores(*pieces):
        return [q for p in pieces for q in (p, swap_cores(p))]

    def forward_chunk(pieces):
        part = jnp.concatenate([forward(hidden, p) for p in pieces], axis=1)
        part = part.astype(jnp.bfloat16)
        return [part, swap_halves(part)]

    def backward_chunk(at, pieces, total):
        for p in pieces:
            total = total + backward(old_grad[:, at * HEAD : (at + 2) * HEAD], p)
            at += 2
        return total

    mixed = mix_layers(depth_pick, depth_coef, old_weights)
    chunk0 = cores(mixed)
    a, b = hop(mixed, mixed)
    grad_part = scatter_blocks(cotangent, out_blocks, out_place, BO_OLD, BO_OLD, True)
    grad_other = swap_halves(grad_part)
    hidden = scatter_blocks(
        attn_out, in_blocks, hidden_place, local_blocks + 1, local_blocks, False
    )
    parts = forward_chunk(chunk0)
    chunk1 = cores(a, b)
    a, b = hop(a, b)
    parts += forward_chunk(chunk1)
    chunk2 = cores(a, b)
    a, b = hop(a, b)
    parts += forward_chunk(chunk2)
    old_grad = add_pair(grad_part, grad_other)
    hidden_grad = backward_chunk(0, chunk0, 0.0)
    hidden_grad = backward_chunk(4, chunk1, hidden_grad)
    chunk3 = cores(a, b)
    half = local_old // 2
    a, b = hop(a[half:], b[:half])
    chunk4 = [(a, b), (swap_cores(a), swap_cores(b))]
    parts += forward_chunk(chunk3)
    hidden_grad = backward_chunk(12, chunk2, hidden_grad)
    hidden_grad = backward_chunk(20, chunk3, hidden_grad)
    parts += forward_chunk(chunk4)
    hidden_grad = backward_chunk(28, chunk4, hidden_grad).astype(jnp.bfloat16)
    hidden_grads = [hidden_grad, swap_halves(hidden_grad)]
    grown_out, keep_out, send_out = width_rows(
        where, out_place, parts, cotangent, out_blocks
    )
    came_out = swap_cores(send_out)
    keep_in, send_in = head_terms(where, in_place, hidden_grads, attn_out)
    came_in = swap_cores(send_in)
    grad_attn = head_grads(where, in_place, hidden_grads, in_blocks)
    grad_scale = float(tok_rows * lax.axis_size(TOKENS)) ** (-0.5)
    full = token_sum((keep_in, keep_out), (came_in, came_out), grad_scale)
    theirs = swap_cores(full)
    sums = unpack_half(where, 0, full, rows_in * HEAD)
    in_sum, out_sum = unpack_half(where, 1, theirs, rows_in * HEAD, sums)
    in_sum = in_sum.reshape(rows_in, 2, HEAD, HEAD)
    out_sum = out_sum.reshape(out_cols.shape[0], 2, HEAD, HEAD)
    return (grown_out, grad_attn, in_sum, out_sum)


def solution(mesh):
    fine = Mesh(mesh.devices.reshape(2, 4, 4, 2, 2, 2), (*TOKENS, "xl"))
    placed = (
        P(TOKENS, None),
        P(TOKENS, "xl"),
        P(None, "xl", (*Z, "c")),
        P(),
        P(),
        P(),
        P(),
        P("xl", None, None, None),
        P("xl", None),
    )
    return jax.shard_map(
        local,
        mesh=fine,
        in_specs=placed,
        out_specs=(
            P(TOKENS, "xl"),
            P(TOKENS, "xl"),
            P("xl", None, None, None),
            P("xl", None, None, None),
        ),
        check_vma=False,
    )
```
